32 devices in a mesh: row: 16 (over z, y, core), col: 2 (over x).
Axes of the slice: x: 2, y: 2, z: 4, core: 2. Of those that a mesh axis runs over, the one named last changes fastest.
Arguments:
- states: bfloat16 [768, 8192], P(None, 'col'), may hold values from -6 to 6
- norm_gain: float32 [8192], P('col'), may hold values from 0.25 to 1.75
- gate_weight: bfloat16 [8192, 28672], P('col', 'row'), may hold values from -0.0625 to 0.0625
- up_weight: bfloat16 [8192, 28672], P('col', 'row'), may hold values from -0.0625 to 0.0625
Outputs:
- near_tiles: float32 [16, 8, 1792, 1792], P('row', 'col')
- far_tiles: float32 [16, 1792, 1792], P('row', 'col')
The draws below stay inside these ranges and needn't reach their ends.
All inputs are finite; a program needn't handle non-finite values.
Results may differ from the reference program's by a relative error of at most 0.0071.
Values may be sent and summed in bfloat16 or wider, within the bound.
A program may use at most 192 MiB of HBM per device.

```python
import jax
import jax.numpy as jnp
from jax import lax

D = 8192
FF = 28672
TOKENS = 768
BLOCK = 1792
N_ROW = 16


def block_levels(stream_key, dims, cuts, smallest, high):
    factor_of = 1.0
    for dim, shards_of in cuts:
        draws = jax.random.uniform(jax.random.fold_in(jax.random.fold_in(stream_key, 6), dim), (shards_of,), jnp.float32, smallest / len(cuts), high / len(cuts))
        factor_of = factor_of * jnp.repeat(jnp.exp(draws), dims[dim] // shards_of).reshape((-1,) + (1,) * (len(dims) - 1 - dim))
    return factor_of


def noise(own_key, dims, spread, bound, split=(), kind=jnp.bfloat16):
    values = jax.random.normal(own_key, dims, jnp.float32) * spread
    if len(split) > 0:
        values = block_levels(own_key, dims, split, -0.22, 0.18) * values
    return jnp.clip(values, min=-bound, max=bound).astype(kind)


def setup_inputs(seed: int = 0) -> dict:
    arg_keys = jax.random.split(jax.random.key(seed), 5)
    states = noise(arg_keys[0], (TOKENS, D), 1.0, 6.0, ((1, 2),))
    norm_gain = jnp.clip(1.0 + 0.15 * jax.random.normal(arg_keys[1], (D,), jnp.float32), 0.25, 1.75)
    gate_weight = noise(arg_keys[2], (D, FF), D ** -0.5, 0.0625, ((0, 2), (1, 16)))
    up_weight = noise(arg_keys[3], (D, FF), D ** -0.5, 0.0625, ((0, 2), (1, 16)))
    return dict(states=states, norm_gain=norm_gain, gate_weight=gate_weight, up_weight=up_weight)


def reference(states, norm_gain, gate_weight, up_weight):
    wide = states.astype(jnp.float32)
    inverse = lax.rsqrt(lax.optimization_barrier(jnp.mean(wide * wide, axis=1)) + 1e-05)
    normed = (wide * inverse[:, None] * norm_gain[None, :]).astype(jnp.bfloat16)
    gate = jnp.dot(normed, gate_weight, preferred_element_type=jnp.float32)
    up = jnp.dot(normed, up_weight, preferred_element_type=jnp.float32)
    keys = (jax.nn.silu(gate) * up).astype(jnp.bfloat16)
    count = keys.shape[0]
    blocks = keys.astype(jnp.float32).reshape(count, N_ROW, BLOCK)
    half = N_ROW // 2

    def one_block(index):
        own = lax.dynamic_index_in_dim(blocks, index, 1, keepdims=False)
        rolled = jnp.roll(blocks, -index, axis=1)
        near = jnp.einsum('tk,tmj->mkj', own, rolled[:, :half], precision=lax.Precision.HIGHEST) / count
        far = jnp.einsum('tk,tj->kj', own, rolled[:, half], precision=lax.Precision.HIGHEST) / count
        return (near, far)
    near_tiles, far_tiles = lax.map(one_block, jnp.arange(N_ROW, dtype=jnp.int32))
    return (near_tiles, far_tiles)
```

```python
import functools

import jax
import jax.numpy as jnp
from jax import lax
from jax.experimental import pallas as pl
from jax.experimental.pallas import tpu as pltpu
from jax.sharding import PartitionSpec as P

LANES = 128
GROUP = 2
MESH = pl.DeviceIdType.MESH
SUM, PAIR, NEXT_OWN, NEXT_OTHER, PREV_OWN, HALF_OWN, HALF_OTHER, SIDE, CORE_ODD, CORE_TOP = range(10)
OWN, STEP, OPPOSITE, BASE1, BASE2, BASE3, BEHIND = range(7)


def passed_along(shard, axis, by):
    devices = lax.axis_size(axis)
    return lax.ppermute(shard, axis, [(i, (i + by) % devices) for i in range(devices)])


def cross(left, right):
    return lax.dot_general(
        left, right, (((0,), (0,)), ((), ())), preferred_element_type=jnp.float32
    )


def gather_kernel(n_row, step, x_ref, gate_hbm, up_hbm, kept, wbuf, partial, sent, got, mine,
                  w_sem, local_sem, send_sem, recv_sem):
    row = lax.axis_index("row")
    col = lax.axis_index("col")
    core = lax.rem(row, 2)
    y = lax.rem(lax.div(row, 2), 2)
    chunks, half, wide = sent.shape
    cut = wide // 2
    group = cut // LANES
    own_rows = pl.ds(pl.multiple_of(col * half, half), half)
    other_rows = pl.ds(pl.multiple_of((1 - col) * half, half), half)

    pair = (row, 1 - col)
    before = (lax.rem(row + n_row - step, n_row), col)
    after = (lax.rem(row + step, n_row), col)
    side = (row + 2 - 4 * y, col)
    twin = (row + 1 - 2 * core, col)

    def weights(j, slot):
        cols = pl.ds(pl.multiple_of(j * cut, cut), cut)
        return (
            pltpu.make_async_copy(gate_hbm.at[:, cols], wbuf.at[slot, :, pl.ds(0, cut)], w_sem.at[slot, 0]),
            pltpu.make_async_copy(up_hbm.at[:, cols], wbuf.at[slot, :, pl.ds(cut, cut)], w_sem.at[slot, 1]),
        )

    def part(slot, j, rows=None):
        where = pl.ds(j * group, group)
        return kept.at[slot, where] if rows is None else kept.at[slot, where, rows]

    def remote(kind, j, src, dst, to):
        return pltpu.make_async_remote_copy(
            src_ref=src, dst_ref=dst, send_sem=send_sem.at[kind, j], recv_sem=recv_sem.at[kind, j],
            device_id=to, device_id_type=MESH,
        )

    def copies(j):
        made = {
            SUM: (sent.at[j], got.at[j], pair),
            PAIR: (mine.at[j], part(OWN, j, own_rows), pair),
            NEXT_OWN: (mine.at[j], part(STEP, j, own_rows), before),
            NEXT_OTHER: (part(OWN, j, other_rows), part(STEP, j, other_rows), before),
            PREV_OWN: (mine.at[j], part(BEHIND, j, own_rows), after),
            HALF_OWN: (part(BEHIND, j, own_rows), part(OPPOSITE, j, own_rows), after),
            HALF_OTHER: (part(STEP, j, other_rows), part(OPPOSITE, j, other_rows), before),
            SIDE: (part(col + 1 - y, j), part(BASE2, j), side),
            CORE_ODD: (part(BASE2 * (1 - core) + col * core, j), part(BASE1, j), twin),
            CORE_TOP: (part((col + 1) * (1 - core) + BASE2 * core, j), part(BASE3, j), twin),
        }
        return {kind: functools.partial(remote, kind, j, *ends) for kind, ends in made.items()}

    def local(j):
        return pltpu.make_async_copy(mine.at[j], part(OWN, j, own_rows), local_sem.at[j])

    for copy in weights(0, 0):
        copy.start()
    barrier = pltpu.get_barrier_semaphore()
    for device in (pair, before, after, side, twin):
        pl.semaphore_signal(barrier, inc=1, device_id=device, device_id_type=MESH)
    pl.semaphore_wait(barrier, 5)

    def stage(t, lag, act):
        j = t - lag

        @pl.when(jnp.logical_and(j >= 0, j < chunks))
        def _():
            act(j, copies(j))

    def multiply(j, copy):
        slot = lax.rem(j, 2)
        for w in weights(j, slot):
            w.wait()

        @pl.when(j + 1 < chunks)
        def _():
            for w in weights(j + 1, 1 - slot):
                w.start()

        sent[j] = jnp.dot(
            x_ref[other_rows, :], wbuf[slot], preferred_element_type=jnp.float32
        ).astype(jnp.bfloat16)
        copy[SUM]().start()
        partial[slot] = jnp.dot(x_ref[own_rows, :], wbuf[slot], preferred_element_type=jnp.float32)

    def activate(j, copy):
        copy[SUM]().wait_recv()
        total = partial[lax.rem(j, 2)] + got[j].astype(jnp.float32)
        gate = total[:, :cut]
        keys = (gate / (1.0 + jnp.exp(-gate)) * total[:, cut:]).astype(jnp.bfloat16)
        for s in range(group):
            mine[j, s] = keys[:, s * LANES:(s + 1) * LANES]
        copy[PAIR]().start()
        copy[NEXT_OWN]().start()
        copy[PREV_OWN]().start()
        local(j).start()

    def spread(j, copy):
        copy[PAIR]().wait_recv()
        copy[NEXT_OTHER]().start()
        copy[PREV_OWN]().wait_recv()
        copy[HALF_OWN]().start()

    def further(j, copy):
        copy[NEXT_OTHER]().wait_recv()
        copy[HALF_OTHER]().start()
        copy[NEXT_OWN]().wait_recv()
        local(j).wait()

    def sideways(j, copy):
        copy[HALF_OWN]().wait_recv()
        copy[HALF_OTHER]().wait_recv()
        copy[SIDE]().start()

    def within(j, copy):
        copy[SIDE]().wait_recv()
        copy[CORE_ODD]().start()
        copy[CORE_TOP]().start()

    def arrive(j, copy):
        copy[CORE_ODD]().wait_recv()
        copy[CORE_TOP]().wait_recv()
        for kind in copy:
            copy[kind]().wait_send()

    @pl.loop(0, chunks + 6)
    def _(t):
        stage(t, 0, multiply)
        stage(t, 1, activate)
        stage(t, 2, spread)
        stage(t, 3, further)
        stage(t, 4, sideways)
        stage(t, 5, within)
        stage(t, 6, arrive)


def gather_keys(n_row, step, normed, gate_weight, up_weight):
    count, depth = normed.shape
    width = gate_weight.shape[1]
    cut = GROUP * LANES
    chunks = width // cut
    half = count // 2
    return pl.pallas_call(
        functools.partial(gather_kernel, n_row, step),
        out_shape=jax.ShapeDtypeStruct((7, width // LANES, count, LANES), jnp.bfloat16),
        in_specs=[
            pl.BlockSpec(memory_space=pltpu.VMEM),
            pl.BlockSpec(memory_space=pl.ANY),
            pl.BlockSpec(memory_space=pl.ANY),
        ],
        out_specs=pl.BlockSpec(memory_space=pl.ANY),
        scratch_shapes=[
            pltpu.VMEM((2, depth, 2 * cut), jnp.bfloat16),
            pltpu.VMEM((2, half, 2 * cut), jnp.float32),
            pltpu.VMEM((chunks, half, 2 * cut), jnp.bfloat16),
            pltpu.VMEM((chunks, half, 2 * cut), jnp.bfloat16),
            pltpu.VMEM((chunks, GROUP, half, LANES), jnp.bfloat16),
            pltpu.SemaphoreType.DMA((2, 2)),
            pltpu.SemaphoreType.DMA((chunks,)),
            pltpu.SemaphoreType.DMA((10, chunks)),
            pltpu.SemaphoreType.DMA((10, chunks)),
        ],
        compiler_params=pltpu.CompilerParams(
            collective_id=0, has_side_effects=True, vmem_limit_bytes=56 * 2**20
        ),
        name="gather_keys",
    )(normed, gate_weight, up_weight)


def tiles_kernel(scale, col_ref, left_ref, right_ref, near_ref, far_ref, turned):
    s = pl.program_id(0)
    last = pl.num_programs(0) - 1
    blocks = left_ref.shape[1]
    slab = far_ref.shape[1]

    @pl.when(s == 0)
    def _():
        for b in range(blocks):
            turned[b * LANES:(b + 1) * LANES, :] = left_ref[0, b].T

    def fill(out_ref, start):
        rows = turned[pl.ds(pl.multiple_of(start, slab), slab), :]
        for b in range(0, blocks, 2):
            right = jnp.concatenate([right_ref[0, b], right_ref[0, b + 1]], axis=1)
            out_ref[:, b * LANES:(b + 2) * LANES] = (
                jnp.dot(rows, right, preferred_element_type=jnp.float32) * scale
            )

    @pl.when(s < last)
    def _():
        fill(near_ref.at[0, 0], lax.rem(s, 2) * slab)

    @pl.when(s == last)
    def _():
        fill(far_ref.at[0], col_ref[0] * slab)


def tiles(kept, col, per_col, scale):
    _, blocks, count, _ = kept.shape
    width = blocks * LANES
    slab = width // 2
    steps = 2 * per_col + 1

    def block_of(s, col_ref):
        m = lax.div(s, 2)
        near = jnp.where(m == 0, col_ref[0], OPPOSITE + m)
        return jnp.where(s == steps - 1, OPPOSITE, near)

    def place_of(s):
        return jnp.minimum(s, steps - 2)

    return pl.pallas_call(
        functools.partial(tiles_kernel, scale),
        grid_spec=pltpu.PrefetchScalarGridSpec(
            num_scalar_prefetch=1,
            grid=(steps,),
            in_specs=[
                pl.BlockSpec((1, blocks, count, LANES), lambda s, c: (OWN, 0, 0, 0)),
                pl.BlockSpec((1, blocks, count, LANES), lambda s, c: (block_of(s, c), 0, 0, 0)),
            ],
            out_specs=[
                pl.BlockSpec((1, 1, slab, width),
                             lambda s, c: (0, lax.div(place_of(s), 2), lax.rem(place_of(s), 2), 0)),
                pl.BlockSpec((1, slab, width), lambda s, c: (0, 0, 0)),
            ],
            scratch_shapes=[pltpu.VMEM((width, count), jnp.bfloat16)],
        ),
        out_shape=(
            jax.ShapeDtypeStruct((1, per_col, width, width), jnp.float32),
            jax.ShapeDtypeStruct((1, slab, width), jnp.float32),
        ),
        compiler_params=pltpu.CompilerParams(
            dimension_semantics=("arbitrary",), vmem_limit_bytes=56 * 2**20
        ),
        name="tiles",
    )(col.reshape(1).astype(jnp.int32), kept, kept)


def by_routes(states, norm_gain, gate_weight, up_weight):
    n_row = lax.axis_size("row")
    n_col = lax.axis_size("col")
    per_col = n_row // (2 * n_col)
    features = states.shape[1] * n_col
    wide = states.astype(jnp.float32)
    squares = lax.psum(jnp.sum(wide * wide, axis=1), "col")
    inverse = lax.rsqrt(squares / features + 1e-05)
    normed = (wide * inverse[:, None] * norm_gain[None, :]).astype(jnp.bfloat16)
    kept = gather_keys(n_row, per_col, normed, gate_weight, up_weight)
    return tiles(kept, lax.axis_index("col"), per_col, 1.0 / states.shape[0])


def on_device(states, norm_gain, gate_weight, up_weight):
    n_row = lax.axis_size("row")
    n_col = lax.axis_size("col")
    column = lax.axis_index("col")
    width = gate_weight.shape[1]
    count = states.shape[0]
    wide = states.astype(jnp.float32)
    squares = lax.psum(jnp.sum(wide * wide, axis=1), "col")
    inverse = lax.rsqrt(squares / (states.shape[1] * n_col) + 1e-05)
    normed = (wide * inverse[:, None] * norm_gain[None, :]).astype(jnp.bfloat16)
    gate_part = jnp.dot(normed, gate_weight, preferred_element_type=jnp.float32)
    up_part = jnp.dot(normed, up_weight, preferred_element_type=jnp.float32)
    summed = lax.psum_scatter(
        jnp.concatenate([gate_part, up_part], axis=1), "col", scatter_dimension=0, tiled=True
    )
    own_keys = (jax.nn.silu(summed[:, :width]) * summed[:, width:]).astype(jnp.bfloat16)
    keys = lax.all_gather(own_keys, "col", axis=0, tiled=True)
    per_col = n_row // (2 * n_col)
    scale = 1.0 / count
    partner = keys
    for target in range(1, n_col):
        arrived = passed_along(keys, "row", n_row - target * per_col)
        partner = jnp.where(column == target, arrived, partner)
    tiles = [cross(keys, partner) * scale]
    for offset in range(1, per_col):
        partner = passed_along(partner, "row", n_row - 1)
        tiles.append(cross(keys, partner) * scale)
    opposite = passed_along(keys, "row", n_row // 2)
    near_tiles = jnp.stack(tiles, axis=0)[None]
    slab = width // n_col
    own_cols = lax.dynamic_slice_in_dim(keys, column * slab, slab, 1)
    far_tiles = (cross(own_cols, opposite) * scale)[None]
    return (near_tiles, far_tiles)


def fits(mesh, states, gate_weight):
    n_row, n_col = mesh.shape["row"], mesh.shape["col"]
    width = gate_weight.shape[1] // n_row
    return n_col == 2 and n_row == 8 * n_col and width % (2 * GROUP * LANES // 2) == 0 and states.shape[0] % 32 == 0


def solution(mesh):
    placed = (P(None, "col"), P("col"), P("col", "row"), P("col", "row"))

    def program(states, norm_gain, gate_weight, up_weight):
        on_each = by_routes if fits(mesh, states, gate_weight) else on_device
        return jax.shard_map(
            on_each,
            mesh=mesh,
            in_specs=placed,
            out_specs=(P("row", "col", None, None), P("row", "col", None)),
            check_vma=False,
        )(states, norm_gain, gate_weight, up_weight)

    return program
```

```python
import functools

import jax
import jax.numpy as jnp
from jax import lax
from jax.experimental import pallas as pl
from jax.experimental.pallas import tpu as pltpu
from jax.sharding import PartitionSpec as P

LANES = 128
GROUP = 1
MESH = pl.DeviceIdType.MESH
(SUM, PAIR, NEXT_OWN, NEXT_OTHER, FAR_OWN, FAR_OTHER, RELAY_OWN, RELAY_OTHER,
 LAST_OWN, LAST_OTHER, SIDE, CORE_ODD, CORE_TOP) = range(13)
OWN, STEP, OPPOSITE, BASE1, BASE2, BASE3 = range(6)


def passed_along(shard, axis, by):
    devices = lax.axis_size(axis)
    return lax.ppermute(shard, axis, [(i, (i + by) % devices) for i in range(devices)])


def cross(left, right):
    return lax.dot_general(
        left, right, (((0,), (0,)), ((), ())), preferred_element_type=jnp.float32
    )


def gather_kernel(n_row, step, x_ref, gate_hbm, up_hbm, kept, wbuf, partial, sent, got, mine,
                  w_sem, local_sem, send_sem, recv_sem):
    row = lax.axis_index("row")
    col = lax.axis_index("col")
    core = lax.rem(row, 2)
    y = lax.rem(lax.div(row, 2), 2)
    chunks, half, wide = sent.shape
    cut = wide // 2
    group = cut // LANES
    own_rows = pl.ds(pl.multiple_of(col * half, half), half)
    other_rows = pl.ds(pl.multiple_of((1 - col) * half, half), half)

    pair = (row, 1 - col)
    level = lax.div(row, step)
    below = (lax.rem(row + n_row - step, n_row), col)
    above = (lax.rem(row + step, n_row), col)
    two_off = (lax.rem(row + 2 * step, n_row), col)
    side = (row + 2 - 4 * y, col)
    twin = (row + 1 - 2 * core, col)

    def weights(j, slot):
        cols = pl.ds(pl.multiple_of(j * cut, cut), cut)
        return (
            pltpu.make_async_copy(gate_hbm.at[:, cols], wbuf.at[slot, :, pl.ds(0, cut)], w_sem.at[slot, 0]),
            pltpu.make_async_copy(up_hbm.at[:, cols], wbuf.at[slot, :, pl.ds(cut, cut)], w_sem.at[slot, 1]),
        )

    def part(slot, j, rows=None):
        where = pl.ds(j * group, group)
        return kept.at[slot, where] if rows is None else kept.at[slot, where, rows]

    def remote(kind, j, src, dst, to):
        return pltpu.make_async_remote_copy(
            src_ref=src, dst_ref=dst, send_sem=send_sem.at[kind, j], recv_sem=recv_sem.at[kind, j],
            device_id=to, device_id_type=MESH,
        )

    def copies(j):
        made = {
            SUM: (sent.at[j], got.at[j], pair),
            PAIR: (mine.at[j], part(OWN, j, own_rows), pair),
            NEXT_OWN: (mine.at[j], part(STEP, j, own_rows), below),
            NEXT_OTHER: (part(OWN, j, other_rows), part(STEP, j, other_rows), below),
            FAR_OWN: (mine.at[j], part(OPPOSITE, j, own_rows), two_off),
            FAR_OTHER: (part(OWN, j, other_rows), part(OPPOSITE, j, other_rows), two_off),
            RELAY_OWN: (part(STEP, j, own_rows), part(OPPOSITE, j, own_rows), below),
            RELAY_OTHER: (part(STEP, j, other_rows), part(OPPOSITE, j, other_rows), below),
            LAST_OWN: (part(OPPOSITE, j, own_rows), part(STEP, j, own_rows), above),
            LAST_OTHER: (part(OPPOSITE, j, other_rows), part(STEP, j, other_rows), above),
            SIDE: (part(col + 1 - y, j), part(BASE2, j), side),
            CORE_ODD: (part(BASE2 * (1 - core) + col * core, j), part(BASE1, j), twin),
            CORE_TOP: (part((col + 1) * (1 - core) + BASE2 * core, j), part(BASE3, j), twin),
        }
        return {kind: functools.partial(remote, kind, j, *ends) for kind, ends in made.items()}

    def local(j):
        return pltpu.make_async_copy(mine.at[j], part(OWN, j, own_rows), local_sem.at[j])

    for copy in weights(0, 0):
        copy.start()
    barrier = pltpu.get_barrier_semaphore()
    for device in (pair, below, above, two_off, side, twin):
        pl.semaphore_signal(barrier, inc=1, device_id=device, device_id_type=MESH)
    pl.semaphore_wait(barrier, 6)

    def stage(t, lag, act):
        j = t - lag

        @pl.when(jnp.logical_and(j >= 0, j < chunks))
        def _():
            act(j, copies(j))

    def multiply(j, copy):
        slot = lax.rem(j, 2)
        for w in weights(j, slot):
            w.wait()

        @pl.when(j + 1 < chunks)
        def _():
            for w in weights(j + 1, 1 - slot):
                w.start()

        sent[j] = jnp.dot(
            x_ref[other_rows, :], wbuf[slot], preferred_element_type=jnp.float32
        ).astype(jnp.bfloat16)
        copy[SUM]().start()
        partial[slot] = jnp.dot(x_ref[own_rows, :], wbuf[slot], preferred_element_type=jnp.float32)

    def activate(j, copy):
        copy[SUM]().wait_recv()
        total = partial[lax.rem(j, 2)] + got[j].astype(jnp.float32)
        gate = total[:, :cut]
        keys = (gate / (1.0 + jnp.exp(-gate)) * total[:, cut:]).astype(jnp.bfloat16)
        for s in range(group):
            mine[j, s] = keys[:, s * LANES:(s + 1) * LANES]
        copy[PAIR]().start()
        start(copy, NEXT_OWN)
        start(copy, FAR_OWN)
        local(j).start()

    senders = {
        NEXT_OWN: level >= 1, NEXT_OTHER: level >= 1,
        FAR_OWN: level <= 1, FAR_OTHER: level <= 1,
        RELAY_OWN: jnp.logical_or(level == 1, level == 2),
        RELAY_OTHER: jnp.logical_or(level == 1, level == 2),
        LAST_OWN: level == 2, LAST_OTHER: level == 2,
    }
    receivers = {
        NEXT_OWN: level <= 2, NEXT_OTHER: level <= 2,
        FAR_OWN: level >= 2, FAR_OTHER: level >= 2,
        RELAY_OWN: level <= 1, RELAY_OTHER: level <= 1,
        LAST_OWN: level == 3, LAST_OTHER: level == 3,
    }

    def start(copy, kind):
        pl.when(senders[kind])(lambda: copy[kind]().start())

    def receive(copy, kind):
        pl.when(receivers[kind])(lambda: copy[kind]().wait_recv())

    def spread(j, copy):
        copy[PAIR]().wait_recv()
        start(copy, NEXT_OTHER)
        start(copy, FAR_OTHER)
        receive(copy, NEXT_OWN)
        start(copy, RELAY_OWN)

    def further(j, copy):
        receive(copy, NEXT_OTHER)
        start(copy, RELAY_OTHER)
        receive(copy, FAR_OWN)
        start(copy, LAST_OWN)

    def onward(j, copy):
        receive(copy, FAR_OTHER)
        start(copy, LAST_OTHER)
        receive(copy, RELAY_OWN)
        local(j).wait()

    def sideways(j, copy):
        receive(copy, RELAY_OTHER)
        receive(copy, LAST_OWN)
        receive(copy, LAST_OTHER)
        copy[SIDE]().start()

    def within(j, copy):
        copy[SIDE]().wait_recv()
        copy[CORE_ODD]().start()
        copy[CORE_TOP]().start()

    def arrive(j, copy):
        copy[CORE_ODD]().wait_recv()
        copy[CORE_TOP]().wait_recv()
        for kind in copy:
            if kind in senders:
                pl.when(senders[kind])(lambda kind=kind: copy[kind]().wait_send())
            else:
                copy[kind]().wait_send()

    @pl.loop(0, chunks + 7)
    def _(t):
        stage(t, 0, multiply)
        stage(t, 1, activate)
        stage(t, 2, spread)
        stage(t, 3, further)
        stage(t, 4, onward)
        stage(t, 5, sideways)
        stage(t, 6, within)
        stage(t, 7, arrive)


def gather_keys(n_row, step, normed, gate_weight, up_weight):
    count, depth = normed.shape
    width = gate_weight.shape[1]
    cut = GROUP * LANES
    chunks = width // cut
    half = count // 2
    return pl.pallas_call(
        functools.partial(gather_kernel, n_row, step),
        out_shape=jax.ShapeDtypeStruct((6, width // LANES, count, LANES), jnp.bfloat16),
        in_specs=[
            pl.BlockSpec(memory_space=pltpu.VMEM),
            pl.BlockSpec(memory_space=pl.ANY),
            pl.BlockSpec(memory_space=pl.ANY),
        ],
        out_specs=pl.BlockSpec(memory_space=pl.ANY),
        scratch_shapes=[
            pltpu.VMEM((2, depth, 2 * cut), jnp.bfloat16),
            pltpu.VMEM((2, half, 2 * cut), jnp.float32),
            pltpu.VMEM((chunks, half, 2 * cut), jnp.bfloat16),
            pltpu.VMEM((chunks, half, 2 * cut), jnp.bfloat16),
            pltpu.VMEM((chunks, GROUP, half, LANES), jnp.bfloat16),
            pltpu.SemaphoreType.DMA((2, 2)),
            pltpu.SemaphoreType.DMA((chunks,)),
            pltpu.SemaphoreType.DMA((13, chunks)),
            pltpu.SemaphoreType.DMA((13, chunks)),
        ],
        compiler_params=pltpu.CompilerParams(
            collective_id=0, has_side_effects=True, vmem_limit_bytes=56 * 2**20
        ),
        name="gather_keys",
    )(normed, gate_weight, up_weight)


def tiles_kernel(scale, col_ref, left_ref, right_ref, near_ref, far_ref, turned):
    s = pl.program_id(0)
    last = pl.num_programs(0) - 1
    blocks = left_ref.shape[1]
    slab = far_ref.shape[1]

    @pl.when(s == 0)
    def _():
        for b in range(blocks):
            turned[b * LANES:(b + 1) * LANES, :] = left_ref[0, b].T

    def fill(out_ref, start):
        rows = turned[pl.ds(pl.multiple_of(start, slab), slab), :]
        for b in range(0, blocks, 2):
            right = jnp.concatenate([right_ref[0, b], right_ref[0, b + 1]], axis=1)
            out_ref[:, b * LANES:(b + 2) * LANES] = (
                jnp.dot(rows, right, preferred_element_type=jnp.float32) * scale
            )

    @pl.when(s < last)
    def _():
        fill(near_ref.at[0, 0], lax.rem(s, 2) * slab)

    @pl.when(s == last)
    def _():
        fill(far_ref.at[0], col_ref[0] * slab)


def tiles(kept, col, per_col, scale):
    _, blocks, count, _ = kept.shape
    width = blocks * LANES
    slab = width // 2
    steps = 2 * per_col + 1

    def block_of(s, col_ref):
        m = lax.div(s, 2)
        near = jnp.where(m == 0, col_ref[0], OPPOSITE + m)
        return jnp.where(s == steps - 1, OPPOSITE, near)

    def place_of(s):
        return jnp.minimum(s, steps - 2)

    return pl.pallas_call(
        functools.partial(tiles_kernel, scale),
        grid_spec=pltpu.PrefetchScalarGridSpec(
            num_scalar_prefetch=1,
            grid=(steps,),
            in_specs=[
                pl.BlockSpec((1, blocks, count, LANES), lambda s, c: (OWN, 0, 0, 0)),
                pl.BlockSpec((1, blocks, count, LANES), lambda s, c: (block_of(s, c), 0, 0, 0)),
            ],
            out_specs=[
                pl.BlockSpec((1, 1, slab, width),
                             lambda s, c: (0, lax.div(place_of(s), 2), lax.rem(place_of(s), 2), 0)),
                pl.BlockSpec((1, slab, width), lambda s, c: (0, 0, 0)),
            ],
            scratch_shapes=[pltpu.VMEM((width, count), jnp.bfloat16)],
        ),
        out_shape=(
            jax.ShapeDtypeStruct((1, per_col, width, width), jnp.float32),
            jax.ShapeDtypeStruct((1, slab, width), jnp.float32),
        ),
        compiler_params=pltpu.CompilerParams(
            dimension_semantics=("arbitrary",), vmem_limit_bytes=56 * 2**20
        ),
        name="tiles",
    )(col.reshape(1).astype(jnp.int32), kept, kept)


def by_routes(states, norm_gain, gate_weight, up_weight):
    n_row = lax.axis_size("row")
    n_col = lax.axis_size("col")
    per_col = n_row // (2 * n_col)
    features = states.shape[1] * n_col
    wide = states.astype(jnp.float32)
    squares = lax.psum(jnp.sum(wide * wide, axis=1), "col")
    inverse = lax.rsqrt(squares / features + 1e-05)
    normed = (wide * inverse[:, None] * norm_gain[None, :]).astype(jnp.bfloat16)
    kept = gather_keys(n_row, per_col, normed, gate_weight, up_weight)
    return tiles(kept, lax.axis_index("col"), per_col, 1.0 / states.shape[0])


def on_device(states, norm_gain, gate_weight, up_weight):
    n_row = lax.axis_size("row")
    n_col = lax.axis_size("col")
    column = lax.axis_index("col")
    width = gate_weight.shape[1]
    count = states.shape[0]
    wide = states.astype(jnp.float32)
    squares = lax.psum(jnp.sum(wide * wide, axis=1), "col")
    inverse = lax.rsqrt(squares / (states.shape[1] * n_col) + 1e-05)
    normed = (wide * inverse[:, None] * norm_gain[None, :]).astype(jnp.bfloat16)
    gate_part = jnp.dot(normed, gate_weight, preferred_element_type=jnp.float32)
    up_part = jnp.dot(normed, up_weight, preferred_element_type=jnp.float32)
    summed = lax.psum_scatter(
        jnp.concatenate([gate_part, up_part], axis=1), "col", scatter_dimension=0, tiled=True
    )
    own_keys = (jax.nn.silu(summed[:, :width]) * summed[:, width:]).astype(jnp.bfloat16)
    keys = lax.all_gather(own_keys, "col", axis=0, tiled=True)
    per_col = n_row // (2 * n_col)
    scale = 1.0 / count
    partner = keys
    for target in range(1, n_col):
        arrived = passed_along(keys, "row", n_row - target * per_col)
        partner = jnp.where(column == target, arrived, partner)
    tiles = [cross(keys, partner) * scale]
    for offset in range(1, per_col):
        partner = passed_along(partner, "row", n_row - 1)
        tiles.append(cross(keys, partner) * scale)
    opposite = passed_along(keys, "row", n_row // 2)
    near_tiles = jnp.stack(tiles, axis=0)[None]
    slab = width // n_col
    own_cols = lax.dynamic_slice_in_dim(keys, column * slab, slab, 1)
    far_tiles = (cross(own_cols, opposite) * scale)[None]
    return (near_tiles, far_tiles)


def fits(mesh, states, gate_weight):
    n_row, n_col = mesh.shape["row"], mesh.shape["col"]
    width = gate_weight.shape[1] // n_row
    return n_col == 2 and n_row == 8 * n_col and width % (2 * LANES) == 0 and states.shape[0] % 32 == 0


def solution(mesh):
    placed = (P(None, "col"), P("col"), P("col", "row"), P("col", "row"))

    def program(states, norm_gain, gate_weight, up_weight):
        on_each = by_routes if fits(mesh, states, gate_weight) else on_device
        return jax.shard_map(
            on_each,
            mesh=mesh,
            in_specs=placed,
            out_specs=(P("row", "col", None, None), P("row", "col", None)),
            check_vma=False,
        )(states, norm_gain, gate_weight, up_weight)

    return program
```

```python
import functools

import jax
import jax.numpy as jnp
from jax import lax
from jax.experimental import pallas as pl
from jax.experimental.pallas import tpu as pltpu
from jax.sharding import PartitionSpec as P

LANES = 128
GROUP = 1
MESH = pl.DeviceIdType.MESH
(SUM, PAIR, NEXT_OWN, NEXT_OTHER, FAR_OWN, FAR_OTHER, RELAY_OWN, RELAY_OTHER,
 LAST_OWN, LAST_OTHER, SIDE, CORE_ODD, CORE_TOP) = range(13)
OWN, STEP, OPPOSITE, BASE1, BASE2, BASE3 = range(6)


def passed_along(shard, axis, by):
    devices = lax.axis_size(axis)
    return lax.ppermute(shard, axis, [(i, (i + by) % devices) for i in range(devices)])


def cross(left, right):
    return lax.dot_general(
        left, right, (((0,), (0,)), ((), ())), preferred_element_type=jnp.float32
    )


def gather_kernel(n_row, step, x_ref, gate_hbm, up_hbm, kept, wbuf, partial, sent, got, mine,
                  w_sem, local_sem, send_sem, recv_sem):
    row = lax.axis_index("row")
    col = lax.axis_index("col")
    core = lax.rem(row, 2)
    y = lax.rem(lax.div(row, 2), 2)
    chunks, half, wide = sent.shape
    cut = wide // 2
    group = cut // LANES
    own_rows = pl.ds(pl.multiple_of(col * half, half), half)
    other_rows = pl.ds(pl.multiple_of((1 - col) * half, half), half)

    pair = (row, 1 - col)
    level = lax.div(row, step)
    below = (lax.rem(row + n_row - step, n_row), col)
    above = (lax.rem(row + step, n_row), col)
    two_off = (lax.rem(row + 2 * step, n_row), col)
    side = (row + 2 - 4 * y, col)
    twin = (row + 1 - 2 * core, col)

    def weights(j, slot):
        cols = pl.ds(pl.multiple_of(j * cut, cut), cut)
        return (
            pltpu.make_async_copy(gate_hbm.at[:, cols], wbuf.at[slot, :, pl.ds(0, cut)], w_sem.at[slot, 0]),
            pltpu.make_async_copy(up_hbm.at[:, cols], wbuf.at[slot, :, pl.ds(cut, cut)], w_sem.at[slot, 1]),
        )

    def part(slot, j, rows=None):
        where = pl.ds(j * group, group)
        return kept.at[slot, where] if rows is None else kept.at[slot, where, rows]

    def remote(kind, j, src, dst, to):
        return pltpu.make_async_remote_copy(
            src_ref=src, dst_ref=dst, send_sem=send_sem.at[kind, j], recv_sem=recv_sem.at[kind, j],
            device_id=to, device_id_type=MESH,
        )

    def copies(j):
        made = {
            SUM: (sent.at[j], got.at[j], pair),
            PAIR: (mine.at[j], part(OWN, j, own_rows), pair),
            NEXT_OWN: (mine.at[j], part(STEP, j, own_rows), below),
            NEXT_OTHER: (part(OWN, j, other_rows), part(STEP, j, other_rows), below),
            FAR_OWN: (mine.at[j], part(OPPOSITE, j, own_rows), two_off),
            FAR_OTHER: (part(OWN, j, other_rows), part(OPPOSITE, j, other_rows), two_off),
            RELAY_OWN: (part(STEP, j, own_rows), part(OPPOSITE, j, own_rows), below),
            RELAY_OTHER: (part(STEP, j, other_rows), part(OPPOSITE, j, other_rows), below),
            LAST_OWN: (part(OPPOSITE, j, own_rows), part(STEP, j, own_rows), above),
            LAST_OTHER: (part(OPPOSITE, j, other_rows), part(STEP, j, other_rows), above),
            SIDE: (part(col + 1 - y, j), part(BASE2, j), side),
            CORE_ODD: (part(BASE2 * (1 - core) + col * core, j), part(BASE1, j), twin),
            CORE_TOP: (part((col + 1) * (1 - core) + BASE2 * core, j), part(BASE3, j), twin),
        }
        return {kind: functools.partial(remote, kind, j, *ends) for kind, ends in made.items()}

    def local(j):
        return pltpu.make_async_copy(mine.at[j], part(OWN, j, own_rows), local_sem.at[j])

    for copy in weights(0, 0):
        copy.start()
    barrier = pltpu.get_barrier_semaphore()
    for device in (pair, below, above, two_off, side, twin):
        pl.semaphore_signal(barrier, inc=1, device_id=device, device_id_type=MESH)
    pl.semaphore_wait(barrier, 6)

    def stage(t, lag, act):
        j = t - lag

        @pl.when(jnp.logical_and(j >= 0, j < chunks))
        def _():
            act(j, copies(j))

    def multiply(j, copy):
        slot = lax.rem(j, 2)
        for w in weights(j, slot):
            w.wait()

        @pl.when(j + 1 < chunks)
        def _():
            for w in weights(j + 1, 1 - slot):
                w.start()

        sent[j] = jnp.dot(
            x_ref[other_rows, :], wbuf[slot], preferred_element_type=jnp.float32
        ).astype(jnp.bfloat16)
        copy[SUM]().start()
        partial[slot] = jnp.dot(x_ref[own_rows, :], wbuf[slot], preferred_element_type=jnp.float32)

    def activate(j, copy):
        copy[SUM]().wait_recv()
        total = partial[lax.rem(j, 2)] + got[j].astype(jnp.float32)
        gate = total[:, :cut]
        keys = (gate / (1.0 + jnp.exp(-gate)) * total[:, cut:]).astype(jnp.bfloat16)
        for s in range(group):
            mine[j, s] = keys[:, s * LANES:(s + 1) * LANES]
        copy[PAIR]().start()
        start(copy, NEXT_OWN)
        start(copy, FAR_OWN)
        local(j).start()

    senders = {
        NEXT_OWN: level >= 1, NEXT_OTHER: level >= 1,
        FAR_OWN: level <= 1, FAR_OTHER: level <= 1,
        RELAY_OWN: jnp.logical_or(level == 1, level == 2),
        RELAY_OTHER: jnp.logical_or(level == 1, level == 2),
        LAST_OWN: level == 2, LAST_OTHER: level == 2,
    }
    receivers = {
        NEXT_OWN: level <= 2, NEXT_OTHER: level <= 2,
        FAR_OWN: level >= 2, FAR_OTHER: level >= 2,
        RELAY_OWN: level <= 1, RELAY_OTHER: level <= 1,
        LAST_OWN: level == 3, LAST_OTHER: level == 3,
    }

    def start(copy, kind):
        pl.when(senders[kind])(lambda: copy[kind]().start())

    def receive(copy, kind):
        pl.when(receivers[kind])(lambda: copy[kind]().wait_recv())

    def spread(j, copy):
        copy[PAIR]().wait_recv()
        start(copy, NEXT_OTHER)
        start(copy, FAR_OTHER)
        receive(copy, NEXT_OWN)
        start(copy, RELAY_OWN)

    def further(j, copy):
        receive(copy, NEXT_OTHER)
        start(copy, RELAY_OTHER)
        receive(copy, FAR_OWN)
        start(copy, LAST_OWN)

    def onward(j, copy):
        receive(copy, FAR_OTHER)
        start(copy, LAST_OTHER)
        receive(copy, RELAY_OWN)
        local(j).wait()

    def sideways(j, copy):
        receive(copy, RELAY_OTHER)
        receive(copy, LAST_OWN)
        receive(copy, LAST_OTHER)
        copy[SIDE]().start()

    def within(j, copy):
        copy[SIDE]().wait_recv()
        copy[CORE_ODD]().start()
        copy[CORE_TOP]().start()

    def arrive(j, copy):
        copy[CORE_ODD]().wait_recv()
        copy[CORE_TOP]().wait_recv()
        for kind in copy:
            if kind in senders:
                pl.when(senders[kind])(lambda kind=kind: copy[kind]().wait_send())
            else:
                copy[kind]().wait_send()

    @pl.loop(0, chunks + 7)
    def _(t):
        stage(t, 0, multiply)
        stage(t, 6, within)
        stage(t, 5, sideways)
        stage(t, 4, onward)
        stage(t, 3, further)
        stage(t, 2, spread)
        stage(t, 1, activate)
        stage(t, 7, arrive)


def gather_keys(n_row, step, normed, gate_weight, up_weight):
    count, depth = normed.shape
    width = gate_weight.shape[1]
    cut = GROUP * LANES
    chunks = width // cut
    half = count // 2
    return pl.pallas_call(
        functools.partial(gather_kernel, n_row, step),
        out_shape=jax.ShapeDtypeStruct((6, width // LANES, count, LANES), jnp.bfloat16),
        in_specs=[
            pl.BlockSpec(memory_space=pltpu.VMEM),
            pl.BlockSpec(memory_space=pl.ANY),
            pl.BlockSpec(memory_space=pl.ANY),
        ],
        out_specs=pl.BlockSpec(memory_space=pl.ANY),
        scratch_shapes=[
            pltpu.VMEM((2, depth, 2 * cut), jnp.bfloat16),
            pltpu.VMEM((2, half, 2 * cut), jnp.float32),
            pltpu.VMEM((chunks, half, 2 * cut), jnp.bfloat16),
            pltpu.VMEM((chunks, half, 2 * cut), jnp.bfloat16),
            pltpu.VMEM((chunks, GROUP, half, LANES), jnp.bfloat16),
            pltpu.SemaphoreType.DMA((2, 2)),
            pltpu.SemaphoreType.DMA((chunks,)),
            pltpu.SemaphoreType.DMA((13, chunks)),
            pltpu.SemaphoreType.DMA((13, chunks)),
        ],
        compiler_params=pltpu.CompilerParams(
            collective_id=0, has_side_effects=True, vmem_limit_bytes=56 * 2**20
        ),
        name="gather_keys",
    )(normed, gate_weight, up_weight)


def tiles_kernel(scale, col_ref, left_ref, right_ref, near_ref, far_ref, turned):
    s = pl.program_id(0)
    last = pl.num_programs(0) - 1
    blocks = left_ref.shape[1]
    slab = far_ref.shape[1]

    @pl.when(s == 0)
    def _():
        for b in range(blocks):
            turned[b * LANES:(b + 1) * LANES, :] = left_ref[0, b].T

    def fill(out_ref, start):
        rows = turned[pl.ds(pl.multiple_of(start, slab), slab), :]
        for b in range(0, blocks, 2):
            right = jnp.concatenate([right_ref[0, b], right_ref[0, b + 1]], axis=1)
            out_ref[:, b * LANES:(b + 2) * LANES] = (
                jnp.dot(rows, right, preferred_element_type=jnp.float32) * scale
            )

    @pl.when(s < last)
    def _():
        fill(near_ref.at[0, 0], lax.rem(s, 2) * slab)

    @pl.when(s == last)
    def _():
        fill(far_ref.at[0], col_ref[0] * slab)


def tiles(kept, col, per_col, scale):
    _, blocks, count, _ = kept.shape
    width = blocks * LANES
    slab = width // 2
    steps = 2 * per_col + 1

    def block_of(s, col_ref):
        m = lax.div(s, 2)
        near = jnp.where(m == 0, col_ref[0], OPPOSITE + m)
        return jnp.where(s == steps - 1, OPPOSITE, near)

    def place_of(s):
        return jnp.minimum(s, steps - 2)

    return pl.pallas_call(
        functools.partial(tiles_kernel, scale),
        grid_spec=pltpu.PrefetchScalarGridSpec(
            num_scalar_prefetch=1,
            grid=(steps,),
            in_specs=[
                pl.BlockSpec((1, blocks, count, LANES), lambda s, c: (OWN, 0, 0, 0)),
                pl.BlockSpec((1, blocks, count, LANES), lambda s, c: (block_of(s, c), 0, 0, 0)),
            ],
            out_specs=[
                pl.BlockSpec((1, 1, slab, width),
                             lambda s, c: (0, lax.div(place_of(s), 2), lax.rem(place_of(s), 2), 0)),
                pl.BlockSpec((1, slab, width), lambda s, c: (0, 0, 0)),
            ],
            scratch_shapes=[pltpu.VMEM((width, count), jnp.bfloat16)],
        ),
        out_shape=(
            jax.ShapeDtypeStruct((1, per_col, width, width), jnp.float32),
            jax.ShapeDtypeStruct((1, slab, width), jnp.float32),
        ),
        compiler_params=pltpu.CompilerParams(
            dimension_semantics=("arbitrary",), vmem_limit_bytes=56 * 2**20
        ),
        name="tiles",
    )(col.reshape(1).astype(jnp.int32), kept, kept)


def by_routes(states, norm_gain, gate_weight, up_weight):
    n_row = lax.axis_size("row")
    n_col = lax.axis_size("col")
    per_col = n_row // (2 * n_col)
    features = states.shape[1] * n_col
    wide = states.astype(jnp.float32)
    squares = lax.psum(jnp.sum(wide * wide, axis=1), "col")
    inverse = lax.rsqrt(squares / features + 1e-05)
    normed = (wide * inverse[:, None] * norm_gain[None, :]).astype(jnp.bfloat16)
    kept = gather_keys(n_row, per_col, normed, gate_weight, up_weight)
    return tiles(kept, lax.axis_index("col"), per_col, 1.0 / states.shape[0])


def on_device(states, norm_gain, gate_weight, up_weight):
    n_row = lax.axis_size("row")
    n_col = lax.axis_size("col")
    column = lax.axis_index("col")
    width = gate_weight.shape[1]
    count = states.shape[0]
    wide = states.astype(jnp.float32)
    squares = lax.psum(jnp.sum(wide * wide, axis=1), "col")
    inverse = lax.rsqrt(squares / (states.shape[1] * n_col) + 1e-05)
    normed = (wide * inverse[:, None] * norm_gain[None, :]).astype(jnp.bfloat16)
    gate_part = jnp.dot(normed, gate_weight, preferred_element_type=jnp.float32)
    up_part = jnp.dot(normed, up_weight, preferred_element_type=jnp.float32)
    summed = lax.psum_scatter(
        jnp.concatenate([gate_part, up_part], axis=1), "col", scatter_dimension=0, tiled=True
    )
    own_keys = (jax.nn.silu(summed[:, :width]) * summed[:, width:]).astype(jnp.bfloat16)
    keys = lax.all_gather(own_keys, "col", axis=0, tiled=True)
    per_col = n_row // (2 * n_col)
    scale = 1.0 / count
    partner = keys
    for target in range(1, n_col):
        arrived = passed_along(keys, "row", n_row - target * per_col)
        partner = jnp.where(column == target, arrived, partner)
    tiles = [cross(keys, partner) * scale]
    for offset in range(1, per_col):
        partner = passed_along(partner, "row", n_row - 1)
        tiles.append(cross(keys, partner) * scale)
    opposite = passed_along(keys, "row", n_row // 2)
    near_tiles = jnp.stack(tiles, axis=0)[None]
    slab = width // n_col
    own_cols = lax.dynamic_slice_in_dim(keys, column * slab, slab, 1)
    far_tiles = (cross(own_cols, opposite) * scale)[None]
    return (near_tiles, far_tiles)


def fits(mesh, states, gate_weight):
    n_row, n_col = mesh.shape["row"], mesh.shape["col"]
    width = gate_weight.shape[1] // n_row
    return n_col == 2 and n_row == 8 * n_col and width % (2 * LANES) == 0 and states.shape[0] % 32 == 0


def solution(mesh):
    placed = (P(None, "col"), P("col"), P("col", "row"), P("col", "row"))

    def program(states, norm_gain, gate_weight, up_weight):
        on_each = by_routes if fits(mesh, states, gate_weight) else on_device
        return jax.shard_map(
            on_each,
            mesh=mesh,
            in_specs=placed,
            out_specs=(P("row", "col", None, None), P("row", "col", None)),
            check_vma=False,
        )(states, norm_gain, gate_weight, up_weight)

    return program
```
